32 devices in a mesh: runs: 2 (over y), ja: 16 (over z, x, core).
Axes of the slice: x: 2, y: 2, z: 4, core: 2. Of those that a mesh axis runs over, the one named last changes fastest.
Arguments:
- pos_vel: float32 [6, 32768], P(None, ('runs', 'ja')), parts along dimension 1, may hold values from -4 to 4
- acc_jerk: float32 [6, 32768], P(None, ('runs', 'ja')), parts along dimension 1, may hold values from -5 to 5
- star_mass: float32 [32768], P(('runs', 'ja')), parts along dimension 0, may hold values from 1.2207031e-05 to 0.00030517578
- step_phase: float32 [32768], P(('runs', 'ja')), parts along dimension 0, may hold values from 0.25 to 1
- step_level: int32 [32768], P(('runs', 'ja')), parts along dimension 0, may hold values from 0 to 3
- counts: int32 [32], P(('runs', 'ja')), parts along dimension 0, may hold values from 1 to 256, 2048 in all
- star_order: int32 [32, 1024], P(('runs', 'ja')), parts along dimension 0, may hold values from 0 to 1023, each once within a row
Outputs:
- new_pos_vel: float32 [6, 32768], P(None, ('runs', 'ja')), parts along dimension 1
- new_acc_jerk: float32 [6, 32768], P(None, ('runs', 'ja')), parts along dimension 1
- active_state: float32 [12, 8192], P(None, ('runs', 'ja')), parts along dimension 1
The draws below stay inside these ranges and needn't reach their ends.
There are 2 independent parts, one for each index of `runs`. The reference program is written for one: setup_inputs(seed, part) draws one part's arguments, and reference() takes and returns one part's arrays. A program takes and returns all parts, laid end to end along the dimension named above; each array names one. Nothing has to cross between parts.
Inputs may be any that keep to these rules, and one draw needn't show every extreme that they name: The counts sum to 2048; the largest is exactly 256. `star_order`: each row is a permutation of the local indices.
All inputs are finite; a program needn't handle non-finite values. No bound on the sum of `counts` on one device may be relied on, other than what follows from the above.
Results may differ from the reference program's by a relative error of at most 0.00002.
Values sent between devices are 32-bit elements; how exact they have to be, the bound alone decides.
A program may use at most 64 MiB of HBM per device.

```python
import math
import jax
import jax.numpy as jnp
import numpy as np
from jax import lax

N_DEV = 1024
CAP = 256
SHARDS = 16
N = 16384
A = 2048


def set_ends(values, own_key, smallest, largest):
    spot = [jax.random.randint(jax.random.fold_in(own_key, axis), (), 0, length) for axis, length in enumerate(values.shape)]
    widest = values.shape.index(max(values.shape))
    next_to = spot[:widest] + [(spot[widest] + 1) % values.shape[widest]] + spot[widest + 1:]
    return values.at[tuple(spot)].set(smallest).at[tuple(next_to)].set(largest)


def block_levels(stream_key, shape, cuts, low, high):
    level = 1.0
    for dim, shards_of in cuts:
        heights = jax.random.uniform(jax.random.fold_in(jax.random.fold_in(stream_key, 6), dim), (shards_of,), jnp.float32, low / len(cuts), high / len(cuts))
        level = level * jnp.repeat(jnp.exp(heights), shape[dim] // shards_of).reshape((-1,) + (1,) * (len(shape) - 1 - dim))
    return level


def split_up(number_of, total, limit, lean):
    portions = [(1 << 20) // math.isqrt(rank ** lean) + 1 for rank in range(2, number_of + 1)]
    surplus, given = total - limit - (number_of - 1), [1] * (number_of - 1)
    while surplus > 0:
        free = [i for i in range(number_of - 1) if given[i] < limit]
        mass, left = sum([portions[i] for i in free]), surplus
        for i in free:
            more = min(limit - given[i], max(1, left * portions[i] // mass), surplus)
            given[i] = given[i] + more
            surplus = surplus - more
    return np.array([limit] + given)


def ragged_sizes(key, count, total, most, lean):
    if count == 2:
        one = jax.random.randint(key, (), max(1, total - most), min(most, total - 1) + 1)
        return jnp.stack([one, total - one])
    sizes = jnp.asarray(split_up(count, total, most, lean), jnp.int32)
    twos = (count - 1) // 2
    donor, sink = sizes[1:1 + 2 * twos:2], sizes[2:2 + 2 * twos:2]
    slack = jnp.minimum(donor - 1, most - sink)
    passed = jax.random.randint(jax.random.fold_in(key, 1), (twos,), 0, 1 << 20) % (slack + 1)
    sizes = sizes.at[1:1 + 2 * twos:2].set(donor - passed).at[2:2 + 2 * twos:2].set(sink + passed)
    return sizes[jax.random.permutation(jax.random.fold_in(key, 2), count)]


def normal_values(key, extent, deviation, bound, cuts=(), kind=jnp.bfloat16):
    drawn = deviation * jax.random.normal(key, extent, jnp.float32)
    if cuts:
        drawn = drawn * block_levels(key, extent, cuts, -0.22, 0.18)
    return jnp.clip(drawn, -bound, bound).astype(kind)


def setup_inputs(seed: int = 0, part: int = 0) -> dict:
    arg_keys = jax.random.split(jax.random.key(seed), 8)
    part_keys = jax.random.split(jax.random.fold_in(arg_keys[7], part), 8)
    return {
        "pos_vel": normal_values(part_keys[0], (6, N), 0.7, 4.0, ((1, 16),), jnp.float32),
        "acc_jerk": normal_values(part_keys[1], (6, N), 1.0, 5.0, ((1, 16),), jnp.float32),
        "star_mass": jnp.clip(jnp.exp(math.log(0.00030517578) - 3.218876 * jax.random.uniform(part_keys[2], (N,), jnp.float32) ** block_levels(part_keys[2], (N,), ((0, 16),), -0.2, 0.2)), 1.220703143189894e-05, 0.00030517578),
        "step_phase": jnp.clip(0.25 + 0.75 * jax.random.uniform(part_keys[3], (N,), jnp.float32) ** block_levels(part_keys[3], (N,), ((0, 16),), -0.2, 0.2), 0.25, 1.0),
        "step_level": set_ends(jax.random.randint(part_keys[4], (N,), 0, 4), jax.random.fold_in(part_keys[4], 1), 0, 3).astype(jnp.int32),
        "counts": ragged_sizes(part_keys[5], SHARDS, A, CAP, 2).astype(jnp.int32),
        "star_order": jax.vmap(lambda own: jax.random.permutation(own, N_DEV))(jax.random.split(part_keys[6], SHARDS)).reshape((SHARDS, N_DEV)).astype(jnp.int32),
    }


soft_sq = 0.01
base_step = 2.0

def predict(pos_vel, acc_jerk, age):
    half_sq = 0.5 * age * age
    sixth_cube = age * age * age / 6.0
    position = pos_vel[0:3] + age * pos_vel[3:6] + half_sq * acc_jerk[0:3] + sixth_cube * acc_jerk[3:6]
    velocity = pos_vel[3:6] + age * acc_jerk[0:3] + half_sq * acc_jerk[3:6]
    return jnp.concatenate([position, velocity], axis=0)

def pair_block(targets, sources):
    delta_x = sources[0:3, None, :] - targets[0:3, :, None]
    delta_v = sources[3:6, None, :] - targets[3:6, :, None]
    dist_sq = soft_sq + delta_x[0] * delta_x[0] + delta_x[1] * delta_x[1] + delta_x[2] * delta_x[2]
    inverse = lax.rsqrt(dist_sq)
    inverse_sq = inverse * inverse
    weight = sources[6][None, :] * inverse * inverse_sq
    radial = 3.0 * (delta_x[0] * delta_v[0] + delta_x[1] * delta_v[1] + delta_x[2] * delta_v[2]) * inverse_sq
    accel_part = lax.optimization_barrier(jnp.sum(weight[None] * delta_x, axis=2))
    jerk_part = lax.optimization_barrier(jnp.sum(weight[None] * (delta_v - radial[None] * delta_x), axis=2))
    return jnp.concatenate([accel_part, jerk_part], axis=0)

def pair_forces(targets, sources, width):
    rows = targets.shape[1]
    block = math.gcd(rows, width)
    split = targets.reshape(6, rows // block, block).transpose(1, 0, 2)
    result = lax.map(lambda part: pair_block(part, sources), split)
    return result.transpose(1, 0, 2).reshape(6, rows)

def correct(old_pv, old_aj, fresh, step_len):
    half = 0.5 * step_len
    twelfth = step_len * step_len / 12.0
    velocity = old_pv[3:6] + half * (old_aj[0:3] + fresh[0:3]) + twelfth * (old_aj[3:6] - fresh[3:6])
    position = old_pv[0:3] + half * (old_pv[3:6] + velocity) + twelfth * (old_aj[0:3] - fresh[0:3])
    return jnp.concatenate([position, velocity], axis=0)

def reference(pos_vel, acc_jerk, star_mass, step_phase, step_level, counts, star_order):
    ends = jnp.cumsum(counts).astype(jnp.int32)
    starts = (ends - counts).astype(jnp.int32)
    place = jnp.arange(A, dtype=jnp.int32)
    owner = jnp.searchsorted(ends, place, side='right').astype(jnp.int32)
    slot = (place - starts[owner]).astype(jnp.int32)
    active_ids = (owner * N_DEV + star_order[owner, slot]).astype(jnp.int32)
    step_len = base_step * jnp.exp2(-step_level.astype(jnp.float32))
    is_active = jnp.zeros((N,), jnp.float32).at[active_ids].set(1.0)
    age = step_len * jnp.where(is_active > 0.5, jnp.float32(1.0), step_phase)
    predicted = predict(pos_vel, acc_jerk, age)
    sources = jnp.concatenate([predicted, star_mass[None, :]], axis=0)
    fresh = pair_forces(predicted[:, active_ids], sources, 256)
    corrected = correct(pos_vel[:, active_ids], acc_jerk[:, active_ids], fresh, step_len[active_ids])
    slot_col = jnp.arange(SHARDS * CAP, dtype=jnp.int32)
    slot_owner = (slot_col // CAP).astype(jnp.int32)
    slot_k = (slot_col - slot_owner * CAP).astype(jnp.int32)
    slot_live = slot_k < counts[slot_owner]
    list_pos = jnp.minimum(starts[slot_owner] + slot_k, A - 1).astype(jnp.int32)
    both = jnp.concatenate([corrected, fresh], axis=0)[:, list_pos]
    active_state = jnp.where(slot_live[None, :], both, jnp.zeros_like(both))
    return (pos_vel.at[:, active_ids].set(corrected), acc_jerk.at[:, active_ids].set(fresh), active_state)
```

```python
import functools

import jax
import jax.numpy as jnp
from jax import lax
from jax.experimental import pallas as pl
from jax.experimental.pallas import tpu as pltpu
from jax.sharding import PartitionSpec as P

A_DEV = 128
CAPACITY = 2 * A_DEV
LANES = 128

soft_sq = 0.01
base_step = 2.0


def step_length(level):
    length = jnp.full(level.shape, base_step, jnp.float32)
    for bit, factor in ((1, 0.5), (2, 0.25), (4, 0.0625)):
        length = length * jnp.where((level & bit) != 0, jnp.float32(factor), jnp.float32(1.0))
    return length


def lane_gather(values, lane):
    return jnp.take_along_axis(values, lane, axis=1)


def gather_from_stars(values, ids):
    group, lane = ids // LANES, ids % LANES
    out = jnp.zeros((8, LANES), jnp.float32)
    for g in range(values.shape[1] // LANES):
        part = lane_gather(values[:, g * LANES : (g + 1) * LANES], lane)
        out = jnp.where(group == g, part, out)
    return out


def correct(old_pv, old_aj, fresh, step_len):
    half = 0.5 * step_len
    twelfth = step_len * step_len * jnp.float32(1.0 / 12.0)
    velocity = (
        old_pv[3:6] + half * (old_aj[0:3] + fresh[0:3]) + twelfth * (old_aj[3:6] - fresh[3:6])
    )
    position = old_pv[0:3] + half * (old_pv[3:6] + velocity) + twelfth * (old_aj[0:3] - fresh[0:3])
    return position, velocity


def kernel(
    n, counts_ref, pv_ref, aj_ref, mass_ref, phase_ref, level_ref, order_ref,
    npv_ref, naj_ref, state_ref,
    srcs, tgts, res, wide, acc, old, slot_row,
    tgt_send, tgt_recv, src_send, src_recv, relay_send, res_send, res_recv,
):
    me = lax.axis_index("ja")
    core, chip, chips = me % 2, me // 2, n // 2
    sibling = me + 1 - 2 * core
    stars = pv_ref.shape[1]

    barrier = pltpu.get_barrier_semaphore()

    def greet(k, carry):
        pl.semaphore_signal(barrier, inc=1, device_id={"ja": (me + k) % n})
        return carry

    lax.fori_loop(1, n, greet, 0)

    count = counts_ref[0]
    order = order_ref[0:1, 0:CAPACITY]
    slots = lax.broadcasted_iota(jnp.int32, (CAPACITY, LANES), 0)
    column = jnp.transpose(jnp.broadcast_to(order.astype(jnp.float32), (8, CAPACITY)))[:, 0:1]
    column = jnp.broadcast_to(column, (CAPACITY, LANES)).astype(jnp.int32)
    column = jnp.where(slots < count, column, -1)
    lanes = lax.broadcasted_iota(jnp.int32, (CAPACITY, LANES), 1)
    for g in range(stars // LANES):
        found = jnp.where(column == lanes + g * LANES, slots, -1)
        slot_row[0:1, g * LANES : (g + 1) * LANES] = jnp.max(found, axis=0, keepdims=True)
    active = slot_row[0:1, :] >= 0

    step_len = step_length(level_ref[...])
    age = step_len * jnp.where(active, jnp.float32(1.0), phase_ref[...])
    half_sq = 0.5 * age * age
    sixth_cube = age * age * age * jnp.float32(1.0 / 6.0)
    pos, vel = pv_ref[0:3, :], pv_ref[3:6, :]
    acl, jrk = aj_ref[0:3, :], aj_ref[3:6, :]
    srcs[me, 0:3, :] = pos + age * vel + half_sq * acl + sixth_cube * jrk
    srcs[me, 3:6, :] = vel + age * acl + half_sq * jrk
    srcs[me, 6:7, :] = mass_ref[...]
    srcs[me, 7:8, :] = step_len

    predicted = srcs[me]
    row = lax.broadcasted_iota(jnp.int32, (8, LANES), 0)
    for h in range(2):
        span = slice(h * LANES, (h + 1) * LANES)
        ids = jnp.broadcast_to(order_ref[0:1, span], (8, LANES))
        got = gather_from_stars(predicted, ids)
        tgts[me, :, span] = jnp.where(row == 6, count.astype(jnp.float32), got)
        old[2, :, span] = got
    tgt_copy = lambda k, o, peer: pltpu.make_async_remote_copy(
        src_ref=tgts.at[o], dst_ref=tgts.at[o], send_sem=tgt_send.at[k], recv_sem=tgt_recv.at[o],
        device_id={"ja": peer},
    )
    src_copy = lambda k, o, peer: pltpu.make_async_remote_copy(
        src_ref=srcs.at[o], dst_ref=srcs.at[o], send_sem=src_send.at[k], recv_sem=src_recv.at[o],
        device_id={"ja": peer},
    )
    relay_copy = lambda k, o: pltpu.make_async_remote_copy(
        src_ref=srcs.at[o], dst_ref=srcs.at[o], send_sem=relay_send.at[k], recv_sem=src_recv.at[o],
        device_id={"ja": sibling},
    )
    res_copy = lambda k, o, peer: pltpu.make_async_remote_copy(
        src_ref=res.at[o], dst_ref=res.at[o], send_sem=res_send.at[k], recv_sem=res_recv.at[o],
        device_id={"ja": peer},
    )

    pl.semaphore_wait(barrier, n - 1)

    def send_targets(k, carry):
        tgt_copy(k, me, (me + k) % n).start()
        return carry

    lax.fori_loop(1, n, send_targets, 0)
    src_copy(0, me, sibling).start()

    def send_sources(j, carry):
        src_copy(j, me, 2 * ((chip + j) % chips) + core).start()
        return carry

    lax.fori_loop(1, chips, send_sources, 0)

    pv_pad = jnp.concatenate([pv_ref[...], jnp.zeros((2, stars), jnp.float32)], axis=0)
    aj_pad = jnp.concatenate([aj_ref[...], jnp.zeros((2, stars), jnp.float32)], axis=0)
    for h in range(2):
        span = slice(h * LANES, (h + 1) * LANES)
        ids = jnp.broadcast_to(order_ref[0:1, span], (8, LANES))
        old[0, :, span] = gather_from_stars(pv_pad, ids)
        old[1, :, span] = gather_from_stars(aj_pad, ids)
    acc[...] = jnp.zeros_like(acc)

    def arrive_targets(k, carry):
        o = (me + n - k) % n
        tgt_copy(k, o, (me + k) % n).wait_recv()
        return carry

    lax.fori_loop(1, n, arrive_targets, 0)

    lane8 = lax.broadcasted_iota(jnp.int32, (8, LANES), 1)

    def pack(o, carry):
        place, mine, packed = carry
        low, high = tgts[o, :, 0:LANES], tgts[o, :, LANES:CAPACITY]
        number = jnp.broadcast_to(low[6:7, :], (8, LANES)).astype(jnp.int32)
        lane = place & (LANES - 1)
        chosen = jnp.where(place < LANES, lane_gather(low, lane), lane_gather(high, lane))
        packed = jnp.where((place >= 0) & (place < number), chosen, packed)
        mine = jnp.where(o == me, 2 * lane8 + me * A_DEV - place, mine)
        return place - number, mine, packed

    _, mine, packed = lax.fori_loop(
        0, n, pack, (lane8 + me * A_DEV, lane8, jnp.zeros((8, LANES), jnp.float32))
    )
    upright = jnp.transpose(packed)
    for c in range(6):
        wide[c, :, :] = jnp.broadcast_to(upright[:, c : c + 1], (A_DEV, LANES))

    def pairs(o):
        def tile(t, carry):
            rows = pl.ds(pl.multiple_of(t * 16, 16), 16)
            at = [wide[c, rows, :] for c in range(6)]
            sums = [acc[c, rows, :] for c in range(9)]
            for g in range(stars // LANES):
                span = slice(g * LANES, (g + 1) * LANES)
                s = [jnp.broadcast_to(srcs[o, c : c + 1, span], (16, LANES)) for c in range(7)]
                dx = [s[c] - at[c] for c in range(3)]
                dv = [s[c + 3] - at[c + 3] for c in range(3)]
                dist_sq = soft_sq + dx[0] * dx[0] + dx[1] * dx[1] + dx[2] * dx[2]
                inverse = lax.rsqrt(dist_sq)
                inverse_sq = inverse * inverse
                weight = s[6] * inverse * inverse_sq
                radial = (dx[0] * dv[0] + dx[1] * dv[1] + dx[2] * dv[2]) * inverse_sq * weight
                for c in range(3):
                    sums[c] = sums[c] + weight * dx[c]
                    sums[c + 3] = sums[c + 3] + weight * dv[c]
                    sums[c + 6] = sums[c + 6] + radial * dx[c]
            for c in range(9):
                acc[c, rows, :] = sums[c]
            return carry

        lax.fori_loop(0, A_DEV // 16, tile, 0)

    pairs(me)

    def visit(j, carry):
        direct = 2 * ((chip + chips - j) % chips) + core
        src_copy(j, direct, direct).wait_recv()
        relay_copy(j, direct).start()
        pairs(direct)
        passed = 2 * ((chip + chips - j + 1) % chips) + 1 - core
        src_copy(0, passed, sibling).wait_recv()
        pairs(passed)
        return carry

    lax.fori_loop(1, chips, visit, 0)
    last = 2 * ((chip + 1) % chips) + 1 - core
    src_copy(0, last, sibling).wait_recv()
    pairs(last)

    ones = jnp.ones((8, LANES), jnp.float32)

    def total(c):
        return lax.dot_general(
            ones, acc[c], (((1,), (1,)), ((), ())), precision=lax.Precision.HIGHEST,
            preferred_element_type=jnp.float32,
        )

    fresh = jnp.zeros((8, LANES), jnp.float32)
    for c in range(3):
        fresh = jnp.where(row == c, total(c), fresh)
        fresh = jnp.where(row == c + 3, total(c + 3) - 3.0 * total(c + 6), fresh)
    res[me] = fresh

    def send_results(k, carry):
        res_copy(k, me, (me + k) % n).start()
        return carry

    lax.fori_loop(1, n, send_results, 0)

    def arrive_results(k, carry):
        o = (me + n - k) % n
        res_copy(k, o, (me + k) % n).wait_recv()
        return carry

    lax.fori_loop(1, n, arrive_results, 0)

    where = [mine + h * LANES for h in range(2)]

    def unpack(o, carry):
        block = res[o]
        return tuple(
            jnp.where(w // LANES == o, lane_gather(block, w % LANES), kept)
            for w, kept in zip(where, carry)
        )

    blank = jnp.zeros((8, LANES), jnp.float32)
    parts = lax.fori_loop(0, n, unpack, (blank, blank))

    for h in range(2):
        span = slice(h * LANES, (h + 1) * LANES)
        live = lane8[0:3] + h * LANES < count
        new_x, new_v = correct(old[0, :, span], old[1, :, span], parts[h], old[2, 7:8, span])
        state_ref[0:3, span] = jnp.where(live, new_x, 0.0)
        state_ref[3:6, span] = jnp.where(live, new_v, 0.0)
        state_ref[6:9, span] = jnp.where(live, parts[h][0:3], 0.0)
        state_ref[9:12, span] = jnp.where(live, parts[h][3:6], 0.0)
    for g in range(stars // LANES):
        span = slice(g * LANES, (g + 1) * LANES)
        slot = jnp.broadcast_to(slot_row[0:1, span], (8, LANES))
        lane = slot & (LANES - 1)
        star = jnp.where(slot < LANES, lane_gather(parts[0], lane), lane_gather(parts[1], lane))
        on = slot[0:3] >= 0
        new_x, new_v = correct(pv_ref[:, span], aj_ref[:, span], star, srcs[me, 7:8, span])
        npv_ref[0:3, span] = jnp.where(on, new_x, pv_ref[0:3, span])
        npv_ref[3:6, span] = jnp.where(on, new_v, pv_ref[3:6, span])
        naj_ref[0:3, span] = jnp.where(on, star[0:3], aj_ref[0:3, span])
        naj_ref[3:6, span] = jnp.where(on, star[3:6], aj_ref[3:6, span])

    def drain(k, carry):
        tgt_copy(k, me, (me + k) % n).wait_send()
        res_copy(k, me, (me + k) % n).wait_send()
        return carry

    lax.fori_loop(1, n, drain, 0)
    src_copy(0, me, sibling).wait_send()

    def drain_sources(j, carry):
        direct = 2 * ((chip + chips - j) % chips) + core
        src_copy(j, me, direct).wait_send()
        relay_copy(j, direct).wait_send()
        return carry

    lax.fori_loop(1, chips, drain_sources, 0)


def per_device(n, pos_vel, acc_jerk, star_mass, step_phase, step_level, counts, star_order):
    stars = pos_vel.shape[1]
    vmem = pl.BlockSpec(memory_space=pltpu.VMEM)
    row = lambda a: a.reshape(1, stars)
    return pl.pallas_call(
        functools.partial(kernel, n),
        out_shape=(
            jax.ShapeDtypeStruct((6, stars), jnp.float32),
            jax.ShapeDtypeStruct((6, stars), jnp.float32),
            jax.ShapeDtypeStruct((12, CAPACITY), jnp.float32),
        ),
        in_specs=[pl.BlockSpec(memory_space=pltpu.SMEM)] + [vmem] * 6,
        out_specs=(vmem, vmem, vmem),
        scratch_shapes=[
            pltpu.VMEM((n, 8, stars), jnp.float32),
            pltpu.VMEM((n, 8, CAPACITY), jnp.float32),
            pltpu.VMEM((n, 8, A_DEV), jnp.float32),
            pltpu.VMEM((6, A_DEV, LANES), jnp.float32),
            pltpu.VMEM((9, A_DEV, LANES), jnp.float32),
            pltpu.VMEM((3, 8, CAPACITY), jnp.float32),
            pltpu.VMEM((8, stars), jnp.int32),
            pltpu.SemaphoreType.DMA((n,)),
            pltpu.SemaphoreType.DMA((n,)),
            pltpu.SemaphoreType.DMA((n,)),
            pltpu.SemaphoreType.DMA((n,)),
            pltpu.SemaphoreType.DMA((n,)),
            pltpu.SemaphoreType.DMA((n,)),
            pltpu.SemaphoreType.DMA((n,)),
        ],
        compiler_params=pltpu.CompilerParams(collective_id=0, has_side_effects=True),
        name="block_step",
    )(counts, pos_vel, acc_jerk, row(star_mass), row(step_phase), row(step_level), star_order)


def solution(mesh):
    n = mesh.shape["ja"]
    in_specs = (
        P(None, ("runs", "ja")),
        P(None, ("runs", "ja")),
        P(("runs", "ja")),
        P(("runs", "ja")),
        P(("runs", "ja")),
        P(("runs", "ja")),
        P(("runs", "ja"), None),
    )
    out_specs = (P(None, ("runs", "ja")), P(None, ("runs", "ja")), P(None, ("runs", "ja")))
    return jax.shard_map(
        functools.partial(per_device, n),
        mesh=mesh, in_specs=in_specs, out_specs=out_specs, check_vma=False,
    )
```

```python
import functools

import jax
import jax.numpy as jnp
from jax import lax
from jax.experimental import pallas as pl
from jax.experimental.pallas import tpu as pltpu
from jax.sharding import PartitionSpec as P

A_DEV = 128
CAPACITY = 2 * A_DEV
LANES = 128

soft_sq = 0.01
base_step = 2.0


def step_length(level):
    length = jnp.full(level.shape, base_step, jnp.float32)
    for bit, factor in ((1, 0.5), (2, 0.25), (4, 0.0625)):
        length = length * jnp.where((level & bit) != 0, jnp.float32(factor), jnp.float32(1.0))
    return length


def lane_gather(values, lane):
    return jnp.take_along_axis(values, lane, axis=1)


def gather_from_stars(values, ids):
    group, lane = ids // LANES, ids % LANES
    out = jnp.zeros((8, LANES), jnp.float32)
    for g in range(values.shape[1] // LANES):
        part = lane_gather(values[:, g * LANES : (g + 1) * LANES], lane)
        out = jnp.where(group == g, part, out)
    return out


def correct(old_pv, old_aj, fresh, step_len):
    half = 0.5 * step_len
    twelfth = step_len * step_len * jnp.float32(1.0 / 12.0)
    velocity = (
        old_pv[3:6] + half * (old_aj[0:3] + fresh[0:3]) + twelfth * (old_aj[3:6] - fresh[3:6])
    )
    position = old_pv[0:3] + half * (old_pv[3:6] + velocity) + twelfth * (old_aj[0:3] - fresh[0:3])
    return position, velocity


def kernel(
    n, counts_ref, pv_ref, aj_ref, mass_ref, phase_ref, level_ref, order_ref,
    npv_ref, naj_ref, state_ref,
    srcs, tgts, res, wide, acc, old, slot_row,
    tgt_send, tgt_recv, src_send, src_recv, relay_send, res_send, res_recv,
):
    me = lax.axis_index("ja")
    core, chip, chips = me % 2, me // 2, n // 2
    sibling = me + 1 - 2 * core
    stars = pv_ref.shape[1]

    barrier = pltpu.get_barrier_semaphore()

    def greet(k, carry):
        pl.semaphore_signal(barrier, inc=1, device_id={"ja": (me + k) % n})
        return carry

    lax.fori_loop(1, n, greet, 0)

    count = jnp.broadcast_to(counts_ref[...], (8, LANES))
    order = order_ref[0:1, 0:CAPACITY]
    slots = lax.broadcasted_iota(jnp.int32, (CAPACITY, LANES), 0)
    column = jnp.transpose(jnp.broadcast_to(order.astype(jnp.float32), (8, CAPACITY)))[:, 0:1]
    column = jnp.broadcast_to(column, (CAPACITY, LANES)).astype(jnp.int32)
    column = jnp.where(slots < jnp.broadcast_to(count[0:1], (CAPACITY, LANES)), column, -1)
    lanes = lax.broadcasted_iota(jnp.int32, (CAPACITY, LANES), 1)
    for g in range(stars // LANES):
        found = jnp.where(column == lanes + g * LANES, slots, -1)
        slot_row[0:1, g * LANES : (g + 1) * LANES] = jnp.max(found, axis=0, keepdims=True)
    active = slot_row[0:1, :] >= 0

    step_len = step_length(level_ref[...])
    age = step_len * jnp.where(active, jnp.float32(1.0), phase_ref[...])
    half_sq = 0.5 * age * age
    sixth_cube = age * age * age * jnp.float32(1.0 / 6.0)
    pos, vel = pv_ref[0:3, :], pv_ref[3:6, :]
    acl, jrk = aj_ref[0:3, :], aj_ref[3:6, :]
    srcs[me, 0:3, :] = pos + age * vel + half_sq * acl + sixth_cube * jrk
    srcs[me, 3:6, :] = vel + age * acl + half_sq * jrk
    srcs[me, 6:7, :] = mass_ref[...]
    srcs[me, 7:8, :] = step_len

    predicted = srcs[me]
    row = lax.broadcasted_iota(jnp.int32, (8, LANES), 0)
    for h in range(2):
        span = slice(h * LANES, (h + 1) * LANES)
        ids = jnp.broadcast_to(order_ref[0:1, span], (8, LANES))
        got = gather_from_stars(predicted, ids)
        tgts[me, :, span] = jnp.where(row == 6, count.astype(jnp.float32), got)
        old[2, :, span] = got
    tgt_copy = lambda k, o, peer: pltpu.make_async_remote_copy(
        src_ref=tgts.at[o], dst_ref=tgts.at[o], send_sem=tgt_send, recv_sem=tgt_recv,
        device_id={"ja": peer},
    )
    src_copy = lambda k, o, peer: pltpu.make_async_remote_copy(
        src_ref=srcs.at[o], dst_ref=srcs.at[o], send_sem=src_send, recv_sem=src_recv.at[o],
        device_id={"ja": peer},
    )
    relay_copy = lambda k, o: pltpu.make_async_remote_copy(
        src_ref=srcs.at[o], dst_ref=srcs.at[o], send_sem=relay_send, recv_sem=src_recv.at[o],
        device_id={"ja": sibling},
    )
    res_copy = lambda k, o, peer: pltpu.make_async_remote_copy(
        src_ref=res.at[o], dst_ref=res.at[o], send_sem=res_send, recv_sem=res_recv,
        device_id={"ja": peer},
    )

    def await_all(ref, number, sem):
        part = ref.at[pl.ds(0, number)]
        pltpu.make_async_copy(part, part, sem).wait()

    pl.semaphore_wait(barrier, n - 1)

    def send_targets(k, carry):
        tgt_copy(k, me, (me + k) % n).start()
        return carry

    lax.fori_loop(1, n, send_targets, 0)
    src_copy(0, me, sibling).start()

    def send_sources(j, carry):
        src_copy(j, me, 2 * ((chip + j) % chips) + core).start()
        return carry

    lax.fori_loop(1, chips, send_sources, 0)

    pv_pad = jnp.concatenate([pv_ref[...], jnp.zeros((2, stars), jnp.float32)], axis=0)
    aj_pad = jnp.concatenate([aj_ref[...], jnp.zeros((2, stars), jnp.float32)], axis=0)
    for h in range(2):
        span = slice(h * LANES, (h + 1) * LANES)
        ids = jnp.broadcast_to(order_ref[0:1, span], (8, LANES))
        old[0, :, span] = gather_from_stars(pv_pad, ids)
        old[1, :, span] = gather_from_stars(aj_pad, ids)
    acc[...] = jnp.zeros_like(acc)

    await_all(tgts, n - 1, tgt_recv)

    lane8 = lax.broadcasted_iota(jnp.int32, (8, LANES), 1)

    def pack(o, carry):
        place, mine, packed = carry
        low, high = tgts[o, :, 0:LANES], tgts[o, :, LANES:CAPACITY]
        number = jnp.broadcast_to(low[6:7, :], (8, LANES)).astype(jnp.int32)
        lane = place & (LANES - 1)
        chosen = jnp.where(place < LANES, lane_gather(low, lane), lane_gather(high, lane))
        packed = jnp.where((place >= 0) & (place < number), chosen, packed)
        mine = jnp.where(o == me, 2 * lane8 + me * A_DEV - place, mine)
        return place - number, mine, packed

    def by_four(step):
        def four(b, carry):
            for k in range(4):
                carry = step(4 * b + k, carry)
            return carry

        return four

    _, mine, packed = lax.fori_loop(
        0, n // 4, by_four(pack), (lane8 + me * A_DEV, lane8, jnp.zeros((8, LANES), jnp.float32))
    )
    upright = jnp.transpose(packed)
    for c in range(6):
        wide[c, :, :] = jnp.broadcast_to(upright[:, c : c + 1], (A_DEV, LANES))

    def pairs(o):
        def tile(t, carry):
            rows = pl.ds(pl.multiple_of(t * 16, 16), 16)
            at = [wide[c, rows, :] for c in range(6)]
            sums = [acc[c, rows, :] for c in range(9)]
            for g in range(stars // LANES):
                span = slice(g * LANES, (g + 1) * LANES)
                s = [jnp.broadcast_to(srcs[o, c : c + 1, span], (16, LANES)) for c in range(7)]
                dx = [s[c] - at[c] for c in range(3)]
                dv = [s[c + 3] - at[c + 3] for c in range(3)]
                dist_sq = soft_sq + dx[0] * dx[0] + dx[1] * dx[1] + dx[2] * dx[2]
                inverse = lax.rsqrt(dist_sq)
                inverse_sq = inverse * inverse
                weight = s[6] * inverse * inverse_sq
                radial = (dx[0] * dv[0] + dx[1] * dv[1] + dx[2] * dv[2]) * inverse_sq
                for c in range(3):
                    pull = weight * dx[c]
                    sums[c] = sums[c] + pull
                    sums[c + 3] = sums[c + 3] + weight * dv[c]
                    sums[c + 6] = sums[c + 6] + radial * pull
            for c in range(9):
                acc[c, rows, :] = sums[c]
            return carry

        lax.fori_loop(0, A_DEV // 16, tile, 0)

    pairs(me)

    def visit(j, carry):
        direct = 2 * ((chip + chips - j) % chips) + core
        src_copy(j, direct, direct).wait_recv()
        relay_copy(j, direct).start()
        pairs(direct)
        passed = 2 * ((chip + chips - j + 1) % chips) + 1 - core
        src_copy(0, passed, sibling).wait_recv()
        pairs(passed)
        return carry

    lax.fori_loop(1, chips, visit, 0)
    last = 2 * ((chip + 1) % chips) + 1 - core
    src_copy(0, last, sibling).wait_recv()
    pairs(last)

    columns = lax.broadcasted_iota(jnp.int32, (A_DEV, LANES), 1)
    upright = jnp.zeros((A_DEV, LANES), jnp.float32)
    for c in range(6):
        part = acc[c] if c < 3 else acc[c] - 3.0 * acc[c + 3]
        upright = jnp.where(columns == c, jnp.sum(part, axis=1, keepdims=True), upright)
    fresh = jnp.transpose(upright)[0:8]
    res[me] = fresh

    def send_results(k, carry):
        res_copy(k, me, (me + k) % n).start()
        return carry

    lax.fori_loop(1, n, send_results, 0)

    await_all(res, n - 1, res_recv)

    where = [mine + h * LANES for h in range(2)]

    def unpack(o, carry):
        block = res[o]
        return tuple(
            jnp.where(w // LANES == o, lane_gather(block, w % LANES), kept)
            for w, kept in zip(where, carry)
        )

    blank = jnp.zeros((8, LANES), jnp.float32)
    parts = lax.fori_loop(0, n // 4, by_four(unpack), (blank, blank))

    for h in range(2):
        span = slice(h * LANES, (h + 1) * LANES)
        live = lane8[0:3] + h * LANES < count[0:3]
        new_x, new_v = correct(old[0, :, span], old[1, :, span], parts[h], old[2, 7:8, span])
        state_ref[0:3, span] = jnp.where(live, new_x, 0.0)
        state_ref[3:6, span] = jnp.where(live, new_v, 0.0)
        state_ref[6:9, span] = jnp.where(live, parts[h][0:3], 0.0)
        state_ref[9:12, span] = jnp.where(live, parts[h][3:6], 0.0)
    for g in range(stars // LANES):
        span = slice(g * LANES, (g + 1) * LANES)
        slot = jnp.broadcast_to(slot_row[0:1, span], (8, LANES))
        lane = slot & (LANES - 1)
        star = jnp.where(slot < LANES, lane_gather(parts[0], lane), lane_gather(parts[1], lane))
        on = slot[0:3] >= 0
        new_x, new_v = correct(pv_ref[:, span], aj_ref[:, span], star, srcs[me, 7:8, span])
        npv_ref[0:3, span] = jnp.where(on, new_x, pv_ref[0:3, span])
        npv_ref[3:6, span] = jnp.where(on, new_v, pv_ref[3:6, span])
        naj_ref[0:3, span] = jnp.where(on, star[0:3], aj_ref[0:3, span])
        naj_ref[3:6, span] = jnp.where(on, star[3:6], aj_ref[3:6, span])

    await_all(tgts, n - 1, tgt_send)
    await_all(res, n - 1, res_send)
    await_all(srcs, chips, src_send)
    await_all(srcs, chips - 1, relay_send)


def per_device(n, pos_vel, acc_jerk, star_mass, step_phase, step_level, counts, star_order):
    stars = pos_vel.shape[1]
    vmem = pl.BlockSpec(memory_space=pltpu.VMEM)
    row = lambda a: a.reshape(1, stars)
    return pl.pallas_call(
        functools.partial(kernel, n),
        out_shape=(
            pltpu.VMEM((6, stars), jnp.float32),
            pltpu.VMEM((6, stars), jnp.float32),
            pltpu.VMEM((12, CAPACITY), jnp.float32),
        ),
        in_specs=[vmem] * 7,
        out_specs=(vmem, vmem, vmem),
        scratch_shapes=[
            pltpu.VMEM((n, 8, stars), jnp.float32),
            pltpu.VMEM((n, 8, CAPACITY), jnp.float32),
            pltpu.VMEM((n, 8, A_DEV), jnp.float32),
            pltpu.VMEM((6, A_DEV, LANES), jnp.float32),
            pltpu.VMEM((9, A_DEV, LANES), jnp.float32),
            pltpu.VMEM((3, 8, CAPACITY), jnp.float32),
            pltpu.VMEM((8, stars), jnp.int32),
            pltpu.SemaphoreType.DMA,
            pltpu.SemaphoreType.DMA,
            pltpu.SemaphoreType.DMA,
            pltpu.SemaphoreType.DMA((n,)),
            pltpu.SemaphoreType.DMA,
            pltpu.SemaphoreType.DMA,
            pltpu.SemaphoreType.DMA,
        ],
        compiler_params=pltpu.CompilerParams(collective_id=0, has_side_effects=True),
        name="block_step",
    )(counts.reshape(1, 1), pos_vel, acc_jerk, row(star_mass), row(step_phase), row(step_level), star_order)


def solution(mesh):
    n = mesh.shape["ja"]
    in_specs = (
        P(None, ("runs", "ja")),
        P(None, ("runs", "ja")),
        P(("runs", "ja")),
        P(("runs", "ja")),
        P(("runs", "ja")),
        P(("runs", "ja")),
        P(("runs", "ja"), None),
    )
    out_specs = (P(None, ("runs", "ja")), P(None, ("runs", "ja")), P(None, ("runs", "ja")))
    return jax.shard_map(
        functools.partial(per_device, n),
        mesh=mesh, in_specs=in_specs, out_specs=out_specs, check_vma=False,
    )
```

```python
import functools

import jax
import jax.numpy as jnp
from jax import lax
from jax.experimental import pallas as pl
from jax.experimental.pallas import tpu as pltpu
from jax.sharding import PartitionSpec as P

A_DEV = 128
CAPACITY = 2 * A_DEV
LANES = 128

soft_sq = 0.01
base_step = 2.0


def step_length(level):
    length = jnp.full(level.shape, base_step, jnp.float32)
    for bit, factor in ((1, 0.5), (2, 0.25), (4, 0.0625)):
        length = length * jnp.where((level & bit) != 0, jnp.float32(factor), jnp.float32(1.0))
    return length


def lane_gather(values, lane):
    return jnp.take_along_axis(values, lane, axis=1)


def gather_from_stars(values, ids):
    group, lane = ids // LANES, ids % LANES
    out = jnp.zeros((8, LANES), jnp.float32)
    for g in range(values.shape[1] // LANES):
        part = lane_gather(values[:, g * LANES : (g + 1) * LANES], lane)
        out = jnp.where(group == g, part, out)
    return out


def correct(old_pv, old_aj, fresh, step_len):
    half = 0.5 * step_len
    twelfth = step_len * step_len * jnp.float32(1.0 / 12.0)
    velocity = (
        old_pv[3:6] + half * (old_aj[0:3] + fresh[0:3]) + twelfth * (old_aj[3:6] - fresh[3:6])
    )
    position = old_pv[0:3] + half * (old_pv[3:6] + velocity) + twelfth * (old_aj[0:3] - fresh[0:3])
    return position, velocity


def kernel(
    n, counts_ref, pv_ref, aj_ref, mass_ref, phase_ref, level_ref, order_ref,
    npv_ref, naj_ref, state_ref,
    srcs, tgts, res, wide, acc, old, slot_row,
    tgt_send, tgt_recv, src_send, src_recv, relay_send, res_send, res_recv,
):
    me = lax.axis_index("ja")
    core, chip, chips = me % 2, me // 2, n // 2
    sibling = me + 1 - 2 * core
    stars = pv_ref.shape[1]

    barrier = pltpu.get_barrier_semaphore()

    def greet(k, carry):
        pl.semaphore_signal(barrier, inc=1, device_id={"ja": (me + k) % n})
        return carry

    lax.fori_loop(1, n, greet, 0)

    count = jnp.broadcast_to(counts_ref[...], (8, LANES))
    order = order_ref[0:1, 0:CAPACITY]
    slots = lax.broadcasted_iota(jnp.int32, (CAPACITY, LANES), 0)
    column = jnp.transpose(jnp.broadcast_to(order.astype(jnp.float32), (8, CAPACITY)))[:, 0:1]
    column = jnp.broadcast_to(column, (CAPACITY, LANES)).astype(jnp.int32)
    column = jnp.where(slots < jnp.broadcast_to(count[0:1], (CAPACITY, LANES)), column, -1)
    lanes = lax.broadcasted_iota(jnp.int32, (CAPACITY, LANES), 1)
    for g in range(stars // LANES):
        found = jnp.where(column == lanes + g * LANES, slots, -1)
        slot_row[0:1, g * LANES : (g + 1) * LANES] = jnp.max(found, axis=0, keepdims=True)
    active = slot_row[0:1, :] >= 0

    step_len = step_length(level_ref[...])
    age = step_len * jnp.where(active, jnp.float32(1.0), phase_ref[...])
    half_sq = 0.5 * age * age
    sixth_cube = age * age * age * jnp.float32(1.0 / 6.0)
    pos, vel = pv_ref[0:3, :], pv_ref[3:6, :]
    acl, jrk = aj_ref[0:3, :], aj_ref[3:6, :]
    srcs[me, 0:3, :] = pos + age * vel + half_sq * acl + sixth_cube * jrk
    srcs[me, 3:6, :] = vel + age * acl + half_sq * jrk
    srcs[me, 6:7, :] = mass_ref[...]
    srcs[me, 7:8, :] = step_len

    predicted = srcs[me]
    row = lax.broadcasted_iota(jnp.int32, (8, LANES), 0)
    for h in range(2):
        span = slice(h * LANES, (h + 1) * LANES)
        ids = jnp.broadcast_to(order_ref[0:1, span], (8, LANES))
        got = gather_from_stars(predicted, ids)
        tgts[me, :, span] = jnp.where(row == 6, count.astype(jnp.float32), got)
        old[2, :, span] = got
    tgt_copy = lambda k, o, peer: pltpu.make_async_remote_copy(
        src_ref=tgts.at[o, pl.ds(0, 7)], dst_ref=tgts.at[o, pl.ds(0, 7)], send_sem=tgt_send, recv_sem=tgt_recv,
        device_id={"ja": peer},
    )
    src_copy = lambda k, o, peer: pltpu.make_async_remote_copy(
        src_ref=srcs.at[o], dst_ref=srcs.at[o], send_sem=src_send, recv_sem=src_recv.at[o],
        device_id={"ja": peer},
    )
    relay_copy = lambda k, o: pltpu.make_async_remote_copy(
        src_ref=srcs.at[o], dst_ref=srcs.at[o], send_sem=relay_send, recv_sem=src_recv.at[o],
        device_id={"ja": sibling},
    )
    res_copy = lambda k, o, peer: pltpu.make_async_remote_copy(
        src_ref=res.at[o, pl.ds(0, 6)], dst_ref=res.at[o, pl.ds(0, 6)], send_sem=res_send, recv_sem=res_recv,
        device_id={"ja": peer},
    )

    def await_all(ref, number, sem, rows=8):
        part = ref.at[pl.ds(0, number), pl.ds(0, rows)]
        pltpu.make_async_copy(part, part, sem).wait()

    pl.semaphore_wait(barrier, n - 1)

    def send_targets(k, carry):
        tgt_copy(k, me, (me + k) % n).start()
        return carry

    lax.fori_loop(1, n, send_targets, 0)
    src_copy(0, me, sibling).start()

    def send_sources(j, carry):
        src_copy(j, me, 2 * ((chip + j) % chips) + core).start()
        return carry

    lax.fori_loop(1, chips, send_sources, 0)

    pv_pad = jnp.concatenate([pv_ref[...], jnp.zeros((2, stars), jnp.float32)], axis=0)
    aj_pad = jnp.concatenate([aj_ref[...], jnp.zeros((2, stars), jnp.float32)], axis=0)
    for h in range(2):
        span = slice(h * LANES, (h + 1) * LANES)
        ids = jnp.broadcast_to(order_ref[0:1, span], (8, LANES))
        old[0, :, span] = gather_from_stars(pv_pad, ids)
        old[1, :, span] = gather_from_stars(aj_pad, ids)
    acc[...] = jnp.zeros_like(acc)

    await_all(tgts, n - 1, tgt_recv, 7)

    lane8 = lax.broadcasted_iota(jnp.int32, (8, LANES), 1)

    def pack(o, carry):
        place, mine, packed = carry
        low, high = tgts[o, :, 0:LANES], tgts[o, :, LANES:CAPACITY]
        number = jnp.broadcast_to(low[6:7, :], (8, LANES)).astype(jnp.int32)
        lane = place & (LANES - 1)
        chosen = jnp.where(place < LANES, lane_gather(low, lane), lane_gather(high, lane))
        packed = jnp.where((place >= 0) & (place < number), chosen, packed)
        mine = jnp.where(o == me, 2 * lane8 + me * A_DEV - place, mine)
        return place - number, mine, packed

    def by_four(step):
        def four(b, carry):
            for k in range(4):
                carry = step(4 * b + k, carry)
            return carry

        return four

    _, mine, packed = lax.fori_loop(
        0, n // 4, by_four(pack), (lane8 + me * A_DEV, lane8, jnp.zeros((8, LANES), jnp.float32))
    )
    upright = jnp.transpose(packed)
    for c in range(6):
        wide[c, :, :] = jnp.broadcast_to(upright[:, c : c + 1], (A_DEV, LANES))

    def pairs(o):
        def tile(t, carry):
            rows = pl.ds(pl.multiple_of(t * 16, 16), 16)
            at = [wide[c, rows, :] for c in range(6)]
            sums = [acc[c, rows, :] for c in range(9)]
            for g in range(stars // LANES):
                span = slice(g * LANES, (g + 1) * LANES)
                s = [jnp.broadcast_to(srcs[o, c : c + 1, span], (16, LANES)) for c in range(7)]
                dx = [s[c] - at[c] for c in range(3)]
                dv = [s[c + 3] - at[c + 3] for c in range(3)]
                dist_sq = soft_sq + dx[0] * dx[0] + dx[1] * dx[1] + dx[2] * dx[2]
                inverse = lax.rsqrt(dist_sq)
                inverse_sq = inverse * inverse
                weight = s[6] * inverse * inverse_sq
                radial = (dx[0] * dv[0] + dx[1] * dv[1] + dx[2] * dv[2]) * inverse_sq
                for c in range(3):
                    pull = weight * dx[c]
                    sums[c] = sums[c] + pull
                    sums[c + 3] = sums[c + 3] + weight * dv[c]
                    sums[c + 6] = sums[c + 6] + radial * pull
            for c in range(9):
                acc[c, rows, :] = sums[c]
            return carry

        def two(b, carry):
            return tile(2 * b + 1, tile(2 * b, carry))

        lax.fori_loop(0, A_DEV // 32, two, 0)

    pairs(me)

    def visit(j, carry):
        direct = 2 * ((chip + chips - j) % chips) + core
        src_copy(j, direct, direct).wait_recv()
        relay_copy(j, direct).start()
        pairs(direct)
        passed = 2 * ((chip + chips - j + 1) % chips) + 1 - core
        src_copy(0, passed, sibling).wait_recv()
        pairs(passed)
        return carry

    lax.fori_loop(1, chips, visit, 0)
    last = 2 * ((chip + 1) % chips) + 1 - core
    src_copy(0, last, sibling).wait_recv()
    pairs(last)

    columns = lax.broadcasted_iota(jnp.int32, (A_DEV, LANES), 1)
    upright = jnp.zeros((A_DEV, LANES), jnp.float32)
    for c in range(6):
        part = acc[c] if c < 3 else acc[c] - 3.0 * acc[c + 3]
        upright = jnp.where(columns == c, jnp.sum(part, axis=1, keepdims=True), upright)
    fresh = jnp.transpose(upright)[0:8]
    res[me] = fresh

    def send_results(k, carry):
        res_copy(k, me, (me + k) % n).start()
        return carry

    lax.fori_loop(1, n, send_results, 0)

    await_all(res, n - 1, res_recv, 6)

    where = [mine + h * LANES for h in range(2)]

    def unpack(o, carry):
        block = res[o]
        return tuple(
            jnp.where(w // LANES == o, lane_gather(block, w % LANES), kept)
            for w, kept in zip(where, carry)
        )

    blank = jnp.zeros((8, LANES), jnp.float32)
    parts = lax.fori_loop(0, n // 4, by_four(unpack), (blank, blank))

    for h in range(2):
        span = slice(h * LANES, (h + 1) * LANES)
        live = lane8[0:3] + h * LANES < count[0:3]
        new_x, new_v = correct(old[0, :, span], old[1, :, span], parts[h], old[2, 7:8, span])
        state_ref[0:3, span] = jnp.where(live, new_x, 0.0)
        state_ref[3:6, span] = jnp.where(live, new_v, 0.0)
        state_ref[6:9, span] = jnp.where(live, parts[h][0:3], 0.0)
        state_ref[9:12, span] = jnp.where(live, parts[h][3:6], 0.0)
    for g in range(stars // LANES):
        span = slice(g * LANES, (g + 1) * LANES)
        slot = jnp.broadcast_to(slot_row[0:1, span], (8, LANES))
        lane = slot & (LANES - 1)
        star = jnp.where(slot < LANES, lane_gather(parts[0], lane), lane_gather(parts[1], lane))
        on = slot[0:3] >= 0
        new_x, new_v = correct(pv_ref[:, span], aj_ref[:, span], star, srcs[me, 7:8, span])
        npv_ref[0:3, span] = jnp.where(on, new_x, pv_ref[0:3, span])
        npv_ref[3:6, span] = jnp.where(on, new_v, pv_ref[3:6, span])
        naj_ref[0:3, span] = jnp.where(on, star[0:3], aj_ref[0:3, span])
        naj_ref[3:6, span] = jnp.where(on, star[3:6], aj_ref[3:6, span])

    await_all(tgts, n - 1, tgt_send, 7)
    await_all(res, n - 1, res_send, 6)
    await_all(srcs, chips, src_send)
    await_all(srcs, chips - 1, relay_send)


def per_device(n, pos_vel, acc_jerk, star_mass, step_phase, step_level, counts, star_order):
    stars = pos_vel.shape[1]
    vmem = pl.BlockSpec(memory_space=pltpu.VMEM)
    row = lambda a: a.reshape(1, stars)
    return pl.pallas_call(
        functools.partial(kernel, n),
        out_shape=(
            pltpu.VMEM((6, stars), jnp.float32),
            pltpu.VMEM((6, stars), jnp.float32),
            pltpu.VMEM((12, CAPACITY), jnp.float32),
        ),
        in_specs=[vmem] * 7,
        out_specs=(vmem, vmem, vmem),
        scratch_shapes=[
            pltpu.VMEM((n, 8, stars), jnp.float32),
            pltpu.VMEM((n, 8, CAPACITY), jnp.float32),
            pltpu.VMEM((n, 8, A_DEV), jnp.float32),
            pltpu.VMEM((6, A_DEV, LANES), jnp.float32),
            pltpu.VMEM((9, A_DEV, LANES), jnp.float32),
            pltpu.VMEM((3, 8, CAPACITY), jnp.float32),
            pltpu.VMEM((8, stars), jnp.int32),
            pltpu.SemaphoreType.DMA,
            pltpu.SemaphoreType.DMA,
            pltpu.SemaphoreType.DMA,
            pltpu.SemaphoreType.DMA((n,)),
            pltpu.SemaphoreType.DMA,
            pltpu.SemaphoreType.DMA,
            pltpu.SemaphoreType.DMA,
        ],
        compiler_params=pltpu.CompilerParams(collective_id=0, has_side_effects=True),
        name="block_step",
    )(counts.reshape(1, 1), pos_vel, acc_jerk, row(star_mass), row(step_phase), row(step_level), star_order)


def solution(mesh):
    n = mesh.shape["ja"]
    in_specs = (
        P(None, ("runs", "ja")),
        P(None, ("runs", "ja")),
        P(("runs", "ja")),
        P(("runs", "ja")),
        P(("runs", "ja")),
        P(("runs", "ja")),
        P(("runs", "ja"), None),
    )
    out_specs = (P(None, ("runs", "ja")), P(None, ("runs", "ja")), P(None, ("runs", "ja")))
    return jax.shard_map(
        functools.partial(per_device, n),
        mesh=mesh, in_specs=in_specs, out_specs=out_specs, check_vma=False,
    )
```

```python
import functools

import jax
import jax.numpy as jnp
from jax import lax
from jax.experimental import pallas as pl
from jax.experimental.pallas import tpu as pltpu
from jax.sharding import PartitionSpec as P

A_DEV = 128
CAPACITY = 2 * A_DEV
LANES = 128

soft_sq = 0.01
base_step = 2.0


def step_length(level):
    length = jnp.full(level.shape, base_step, jnp.float32)
    for bit, factor in ((1, 0.5), (2, 0.25), (4, 0.0625)):
        length = length * jnp.where((level & bit) != 0, jnp.float32(factor), jnp.float32(1.0))
    return length


def lane_gather(values, lane):
    return jnp.take_along_axis(values, lane, axis=1)


def gather_from_stars(values, ids):
    group, lane = ids // LANES, ids % LANES
    out = jnp.zeros((8, LANES), jnp.float32)
    for g in range(values.shape[1] // LANES):
        part = lane_gather(values[:, g * LANES : (g + 1) * LANES], lane)
        out = jnp.where(group == g, part, out)
    return out


def correct(old_pv, old_aj, fresh, step_len):
    half = 0.5 * step_len
    twelfth = step_len * step_len * jnp.float32(1.0 / 12.0)
    velocity = (
        old_pv[3:6] + half * (old_aj[0:3] + fresh[0:3]) + twelfth * (old_aj[3:6] - fresh[3:6])
    )
    position = old_pv[0:3] + half * (old_pv[3:6] + velocity) + twelfth * (old_aj[0:3] - fresh[0:3])
    return position, velocity


def kernel(
    n, counts_ref, pv_ref, aj_ref, mass_ref, phase_ref, level_ref, order_ref,
    npv_ref, naj_ref, state_ref,
    srcs, tgts, res, wide, acc, old, slot_row,
    tgt_send, tgt_recv, src_send, src_recv, relay_send, res_send, res_recv,
):
    me = lax.axis_index("ja")
    core, chip, chips = me % 2, me // 2, n // 2
    sibling = me + 1 - 2 * core
    stars = pv_ref.shape[1]

    barrier = pltpu.get_barrier_semaphore()

    def greet(k, carry):
        pl.semaphore_signal(barrier, inc=1, device_id={"ja": (me + k) % n})
        return carry

    lax.fori_loop(1, n, greet, 0)

    count = jnp.broadcast_to(counts_ref[...], (8, LANES))
    order = order_ref[0:1, 0:CAPACITY]
    slots = lax.broadcasted_iota(jnp.int32, (CAPACITY, LANES), 0)
    column = jnp.transpose(jnp.broadcast_to(order.astype(jnp.float32), (8, CAPACITY)))[:, 0:1]
    column = jnp.broadcast_to(column, (CAPACITY, LANES)).astype(jnp.int32)
    column = jnp.where(slots < jnp.broadcast_to(count[0:1], (CAPACITY, LANES)), column, -1)
    lanes = lax.broadcasted_iota(jnp.int32, (CAPACITY, LANES), 1)
    for g in range(stars // LANES):
        found = jnp.where(column == lanes + g * LANES, slots, -1)
        slot_row[0:1, g * LANES : (g + 1) * LANES] = jnp.max(found, axis=0, keepdims=True)
    active = slot_row[0:1, :] >= 0

    step_len = step_length(level_ref[...])
    age = step_len * jnp.where(active, jnp.float32(1.0), phase_ref[...])
    half_sq = 0.5 * age * age
    sixth_cube = age * age * age * jnp.float32(1.0 / 6.0)
    pos, vel = pv_ref[0:3, :], pv_ref[3:6, :]
    acl, jrk = aj_ref[0:3, :], aj_ref[3:6, :]
    srcs[me, 0:3, :] = pos + age * vel + half_sq * acl + sixth_cube * jrk
    srcs[me, 3:6, :] = vel + age * acl + half_sq * jrk
    srcs[me, 6:7, :] = mass_ref[...]
    srcs[me, 7:8, :] = step_len

    predicted = srcs[me]
    row = lax.broadcasted_iota(jnp.int32, (8, LANES), 0)
    for h in range(2):
        span = slice(h * LANES, (h + 1) * LANES)
        ids = jnp.broadcast_to(order_ref[0:1, span], (8, LANES))
        got = gather_from_stars(predicted, ids)
        tgts[me, :, span] = jnp.where(row == 6, count.astype(jnp.float32), got)
        old[2, :, span] = got
    tgt_copy = lambda k, o, peer: pltpu.make_async_remote_copy(
        src_ref=tgts.at[o, pl.ds(0, 7)], dst_ref=tgts.at[o, pl.ds(0, 7)], send_sem=tgt_send, recv_sem=tgt_recv,
        device_id={"ja": peer},
    )
    src_copy = lambda k, o, peer: pltpu.make_async_remote_copy(
        src_ref=srcs.at[o], dst_ref=srcs.at[o], send_sem=src_send, recv_sem=src_recv.at[o],
        device_id={"ja": peer},
    )
    relay_copy = lambda k, o: pltpu.make_async_remote_copy(
        src_ref=srcs.at[o], dst_ref=srcs.at[o], send_sem=relay_send, recv_sem=src_recv.at[o],
        device_id={"ja": sibling},
    )
    res_copy = lambda k, o, peer: pltpu.make_async_remote_copy(
        src_ref=res.at[o, pl.ds(0, 6)], dst_ref=res.at[o, pl.ds(0, 6)], send_sem=res_send, recv_sem=res_recv,
        device_id={"ja": peer},
    )

    def await_all(ref, number, sem, rows=8):
        part = ref.at[pl.ds(0, number), pl.ds(0, rows)]
        pltpu.make_async_copy(part, part, sem).wait()

    pl.semaphore_wait(barrier, n - 1)

    def send_targets(k, carry):
        tgt_copy(k, me, (me + k) % n).start()
        return carry

    lax.fori_loop(1, n, send_targets, 0)
    src_copy(0, me, sibling).start()

    def send_sources(j, carry):
        src_copy(j, me, 2 * ((chip + j) % chips) + core).start()
        return carry

    lax.fori_loop(1, chips, send_sources, 0)

    pv_pad = jnp.concatenate([pv_ref[...], jnp.zeros((2, stars), jnp.float32)], axis=0)
    aj_pad = jnp.concatenate([aj_ref[...], jnp.zeros((2, stars), jnp.float32)], axis=0)
    for h in range(2):
        span = slice(h * LANES, (h + 1) * LANES)
        ids = jnp.broadcast_to(order_ref[0:1, span], (8, LANES))
        old[0, :, span] = gather_from_stars(pv_pad, ids)
        old[1, :, span] = gather_from_stars(aj_pad, ids)
    acc[...] = jnp.zeros_like(acc)

    await_all(tgts, n - 1, tgt_recv, 7)

    lane8 = lax.broadcasted_iota(jnp.int32, (8, LANES), 1)

    def pack(o, carry):
        place, mine, packed = carry
        low, high = tgts[o, :, 0:LANES], tgts[o, :, LANES:CAPACITY]
        number = jnp.broadcast_to(low[6:7, :], (8, LANES)).astype(jnp.int32)
        lane = place & (LANES - 1)
        chosen = jnp.where(place < LANES, lane_gather(low, lane), lane_gather(high, lane))
        packed = jnp.where((place >= 0) & (place < number), chosen, packed)
        mine = jnp.where(o == me, 2 * lane8 + me * A_DEV - place, mine)
        return place - number, mine, packed

    def by_four(step):
        def four(b, carry):
            for k in range(4):
                carry = step(4 * b + k, carry)
            return carry

        return four

    _, mine, packed = lax.fori_loop(
        0, n // 4, by_four(pack), (lane8 + me * A_DEV, lane8, jnp.zeros((8, LANES), jnp.float32))
    )
    upright = jnp.transpose(packed)
    for c in range(6):
        wide[c, :, :] = jnp.broadcast_to(upright[:, c : c + 1], (A_DEV, LANES))

    def pairs(o):
        def tile(t, carry):
            rows = pl.ds(pl.multiple_of(t * 16, 16), 16)
            at = [wide[c, rows, :] for c in range(6)]
            sums = [acc[c, rows, :] for c in range(9)]
            for g in range(stars // LANES):
                span = slice(g * LANES, (g + 1) * LANES)
                s = [jnp.broadcast_to(srcs[o, c : c + 1, span], (16, LANES)) for c in range(7)]
                dx = [s[c] - at[c] for c in range(3)]
                dv = [s[c + 3] - at[c + 3] for c in range(3)]
                dist_sq = soft_sq + dx[0] * dx[0] + dx[1] * dx[1] + dx[2] * dx[2]
                inverse = lax.rsqrt(dist_sq)
                inverse_sq = inverse * inverse
                weight = s[6] * inverse * inverse_sq
                radial = (dx[0] * dv[0] + dx[1] * dv[1] + dx[2] * dv[2]) * inverse_sq
                for c in range(3):
                    pull = weight * dx[c]
                    sums[c] = sums[c] + pull
                    sums[c + 3] = sums[c + 3] + weight * dv[c]
                    sums[c + 6] = sums[c + 6] + radial * pull
            for c in range(9):
                acc[c, rows, :] = sums[c]
            return carry

        def four_tiles(b, carry):
            for k in range(4):
                tile(4 * b + k, carry)
            return carry

        lax.fori_loop(0, A_DEV // 64, four_tiles, 0)

    pairs(me)

    def visit(j, carry):
        direct = 2 * ((chip + chips - j) % chips) + core
        src_copy(j, direct, direct).wait_recv()
        relay_copy(j, direct).start()
        pairs(direct)
        passed = 2 * ((chip + chips - j + 1) % chips) + 1 - core
        src_copy(0, passed, sibling).wait_recv()
        pairs(passed)
        return carry

    lax.fori_loop(1, chips, visit, 0)
    last = 2 * ((chip + 1) % chips) + 1 - core
    src_copy(0, last, sibling).wait_recv()
    pairs(last)

    columns = lax.broadcasted_iota(jnp.int32, (A_DEV, LANES), 1)
    upright = jnp.zeros((A_DEV, LANES), jnp.float32)
    for c in range(6):
        part = acc[c] if c < 3 else acc[c] - 3.0 * acc[c + 3]
        upright = jnp.where(columns == c, jnp.sum(part, axis=1, keepdims=True), upright)
    fresh = jnp.transpose(upright)[0:8]
    res[me] = fresh

    def send_results(k, carry):
        res_copy(k, me, (me + k) % n).start()
        return carry

    lax.fori_loop(1, n, send_results, 0)

    await_all(res, n - 1, res_recv, 6)

    where = [mine + h * LANES for h in range(2)]

    def unpack(o, carry):
        block = res[o]
        return tuple(
            jnp.where(w // LANES == o, lane_gather(block, w % LANES), kept)
            for w, kept in zip(where, carry)
        )

    blank = jnp.zeros((8, LANES), jnp.float32)
    parts = lax.fori_loop(0, n // 4, by_four(unpack), (blank, blank))

    for h in range(2):
        span = slice(h * LANES, (h + 1) * LANES)
        live = lane8[0:3] + h * LANES < count[0:3]
        new_x, new_v = correct(old[0, :, span], old[1, :, span], parts[h], old[2, 7:8, span])
        state_ref[0:3, span] = jnp.where(live, new_x, 0.0)
        state_ref[3:6, span] = jnp.where(live, new_v, 0.0)
        state_ref[6:9, span] = jnp.where(live, parts[h][0:3], 0.0)
        state_ref[9:12, span] = jnp.where(live, parts[h][3:6], 0.0)
    for g in range(stars // LANES):
        span = slice(g * LANES, (g + 1) * LANES)
        slot = jnp.broadcast_to(slot_row[0:1, span], (8, LANES))
        lane = slot & (LANES - 1)
        star = jnp.where(slot < LANES, lane_gather(parts[0], lane), lane_gather(parts[1], lane))
        on = slot[0:3] >= 0
        new_x, new_v = correct(pv_ref[:, span], aj_ref[:, span], star, srcs[me, 7:8, span])
        npv_ref[0:3, span] = jnp.where(on, new_x, pv_ref[0:3, span])
        npv_ref[3:6, span] = jnp.where(on, new_v, pv_ref[3:6, span])
        naj_ref[0:3, span] = jnp.where(on, star[0:3], aj_ref[0:3, span])
        naj_ref[3:6, span] = jnp.where(on, star[3:6], aj_ref[3:6, span])

    await_all(tgts, n - 1, tgt_send, 7)
    await_all(res, n - 1, res_send, 6)
    await_all(srcs, chips, src_send)
    await_all(srcs, chips - 1, relay_send)


def per_device(n, pos_vel, acc_jerk, star_mass, step_phase, step_level, counts, star_order):
    stars = pos_vel.shape[1]
    vmem = pl.BlockSpec(memory_space=pltpu.VMEM)
    row = lambda a: a.reshape(1, stars)
    return pl.pallas_call(
        functools.partial(kernel, n),
        out_shape=(
            pltpu.VMEM((6, stars), jnp.float32),
            pltpu.VMEM((6, stars), jnp.float32),
            pltpu.VMEM((12, CAPACITY), jnp.float32),
        ),
        in_specs=[vmem] * 7,
        out_specs=(vmem, vmem, vmem),
        scratch_shapes=[
            pltpu.VMEM((n, 8, stars), jnp.float32),
            pltpu.VMEM((n, 8, CAPACITY), jnp.float32),
            pltpu.VMEM((n, 8, A_DEV), jnp.float32),
            pltpu.VMEM((6, A_DEV, LANES), jnp.float32),
            pltpu.VMEM((9, A_DEV, LANES), jnp.float32),
            pltpu.VMEM((3, 8, CAPACITY), jnp.float32),
            pltpu.VMEM((8, stars), jnp.int32),
            pltpu.SemaphoreType.DMA,
            pltpu.SemaphoreType.DMA,
            pltpu.SemaphoreType.DMA,
            pltpu.SemaphoreType.DMA((n,)),
            pltpu.SemaphoreType.DMA,
            pltpu.SemaphoreType.DMA,
            pltpu.SemaphoreType.DMA,
        ],
        compiler_params=pltpu.CompilerParams(collective_id=0, has_side_effects=True),
        name="block_step",
    )(counts.reshape(1, 1), pos_vel, acc_jerk, row(star_mass), row(step_phase), row(step_level), star_order)


def solution(mesh):
    n = mesh.shape["ja"]
    in_specs = (
        P(None, ("runs", "ja")),
        P(None, ("runs", "ja")),
        P(("runs", "ja")),
        P(("runs", "ja")),
        P(("runs", "ja")),
        P(("runs", "ja")),
        P(("runs", "ja"), None),
    )
    out_specs = (P(None, ("runs", "ja")), P(None, ("runs", "ja")), P(None, ("runs", "ja")))
    return jax.shard_map(
        functools.partial(per_device, n),
        mesh=mesh, in_specs=in_specs, out_specs=out_specs, check_vma=False,
    )
```
